32 devices in a mesh: half: 1, grp: 4 (over y, core), dev: 8 (over z, x).
Axes of the slice: x: 2, y: 2, z: 4, core: 2. Of those that a mesh axis runs over, the one named last changes fastest.
Arguments:
- panel_block: float32 [2048, 512], P(('half', 'grp', 'dev')), may hold values from -1 to 1, as said below
- trailing: float32 [2048, 1024], P(('half', 'grp'), 'dev'), may hold values from -6 to 6
Outputs:
- triangle: float32 [512, 512], replicated
- projected: float32 [512, 1024], P(None, 'dev')
- remainder: float32 [2048, 1024], P(('half', 'grp'), 'dev')
The draws below stay inside these ranges and needn't reach their ends.
Inputs may be any that keep to these rules, and one draw needn't show every extreme that they name: `panel_block`: of full column rank.
All inputs are finite; a program needn't handle non-finite values.
Results may differ from the reference program's by a relative error of at most 0.0003.
Values sent between devices are 32-bit elements; how exact they have to be, the bound alone decides.
A program may use at most 64 MiB of HBM per device.

```python
import jax
import jax.numpy as jnp
from jax import lax

P_SIZE = 512
ROWS = 2048
SLAB = 1024


def draw_panel_block(key, part):
    first = jax.random.fold_in(key, 11)
    second = jax.random.fold_in(key, 23)
    values = jnp.clip(jax.random.normal(first, (ROWS, P_SIZE), jnp.float32), -6.0, 6.0)
    position = jnp.arange(ROWS, dtype=jnp.float32) / ROWS
    row_scale = (3.0 ** position)[:, None] * jax.random.uniform(second, (ROWS, 1), jnp.float32, 0.7, 1.3)
    values = values * row_scale / jnp.sqrt(jnp.float32(ROWS))
    return jnp.clip(values, -1.0, 1.0)


def block_scale(rng, extent, split, least, largest):
    factor_of = 1.0
    for dim, blocks in split:
        steps = jax.random.uniform(jax.random.fold_in(jax.random.fold_in(rng, 6), dim), (blocks,), jnp.float32, least / len(split), largest / len(split))
        factor_of = factor_of * jnp.repeat(jnp.exp(steps), extent[dim] // blocks).reshape((-1,) + (1,) * (len(extent) - 1 - dim))
    return factor_of


def normal_values(stream_key, extent, width, limit, pieces=(), kind=jnp.bfloat16):
    gain = block_scale(stream_key, extent, pieces, -0.22, 0.18) if pieces else 1.0
    values = jax.random.normal(stream_key, extent, jnp.float32) * width * gain
    return jnp.minimum(jnp.maximum(values, -limit), limit).astype(kind)


def setup_inputs(seed: int = 0) -> dict:
    arg_keys = jax.random.split(jax.random.key(seed), 3)
    panel_block = draw_panel_block(jax.random.fold_in(arg_keys[2], 71), 0)
    trailing = normal_values(arg_keys[1], (ROWS, SLAB), 1.0, 6.0, ((0, 4), (1, 8)), jnp.float32)
    return {"panel_block": panel_block, "trailing": trailing}


def reference(panel_block, trailing):
    orthonormal, upper_part = jnp.linalg.qr(panel_block)
    signs = jnp.sign(jnp.diagonal(upper_part))
    triangle = upper_part * signs[:, None]
    orthonormal = orthonormal * signs[None, :]
    projected = jnp.dot(orthonormal.T, trailing, precision=lax.Precision.HIGHEST)
    remainder = trailing - jnp.dot(orthonormal, projected, precision=lax.Precision.HIGHEST)
    return (triangle, projected, remainder)
```

```python
import functools

import jax
import jax.numpy as jnp
from jax import lax
from jax.experimental import pallas as pl
from jax.experimental.pallas import tpu as pltpu
from jax.sharding import PartitionSpec as P

HIGHEST = lax.Precision.HIGHEST
NB = 128
SUB = 8


def dot(a, b):
    return jnp.dot(a, b, precision=HIGHEST, preferred_element_type=jnp.float32)


def dot_t(a, b):
    return lax.dot_general(
        a, b, (((0,), (0,)), ((), ())), precision=HIGHEST,
        preferred_element_type=jnp.float32,
    )


def factor_block(block, upper_ref, inverse_ref, row0, col0):
    tile = (SUB, NB)
    lane = lax.broadcasted_iota(jnp.int32, tile, 1)
    zero = jnp.zeros(tile, jnp.float32)
    groups = len(block)
    block = list(block)
    for b in range(groups):
        c0 = SUB * b
        own = block[b]
        marks = [lane == c0 + t for t in range(SUB)]
        inside = (lane >= c0) & (lane < c0 + SUB)
        after = lane >= c0 + SUB
        rows = [jnp.broadcast_to(own[s:s + 1, :], tile) for s in range(SUB)]
        d = {}
        for s in range(SUB):
            for t in range(s, SUB):
                d[s, t] = jnp.broadcast_to(rows[s][:, c0 + t:c0 + t + 1], tile)
        columns = [
            [jnp.broadcast_to(block[g][:, c0 + t:c0 + t + 1], tile) for t in range(SUB)]
            for g in range(b + 1, groups)
        ]
        v = []
        for s in range(SUB):
            unit = jnp.where(marks[s], 1.0, 0.0)
            v.append(jnp.where(inside, unit, rows[s]))
        for j in range(SUB):
            rs = lax.rsqrt(d[j, j])
            u = {k: d[j, k] * rs for k in range(j, SUB)}
            vs = v[j] * rs
            up = jnp.where(after, vs, zero)
            for k in range(j, SUB):
                up = jnp.where(marks[k], u[k], up)
            low = jnp.where(after, zero, vs)
            upper_ref[row0 + c0 + j:row0 + c0 + j + 1, col0:col0 + NB] = up[0:1, :]
            inverse_ref[row0 + c0 + j:row0 + c0 + j + 1, :] = low[0:1, :]
            for i in range(SUB):
                if i == j:
                    continue
                e = u[i] if i > j else d[i, j] * rs
                v[i] = v[i] - e * vs
                for k in range(max(j + 1, i), SUB):
                    d[i, k] = d[i, k] - e * u[k]
            v[j] = vs * rs
            for k in range(j + 1, SUB):
                d[j, k] = u[k] * rs
        for g in range(b + 1, groups):
            terms = [columns[g - b - 1][t] * v[t] for t in range(SUB)]
            while len(terms) > 1:
                terms = [terms[i] + terms[i + 1] for i in range(0, len(terms), 2)]
            block[g] = jnp.where(inside, zero, block[g]) - terms[0]


def solve_kernel(panel_ref, gram_ref, cross_ref, trailing_ref, triangle_ref, projected_ref,
                 remainder_ref, gram, cross, inverse, solved, corner, upper, lower):
    p = gram_ref.shape[0]
    blocks = p // NB
    gram[...] = gram_ref[...]
    cross[...] = cross_ref[...]
    def step(index, carry):
        start = pl.multiple_of(index * NB, NB)
        corner[...] = gram[pl.ds(start, NB), pl.ds(start, NB)]
        rows = [corner[SUB * g:SUB * (g + 1), :] for g in range(NB // SUB)]
        factor_block(rows, upper, lower, 0, 0)
        for k in range(blocks):
            pl.when(index == k)(functools.partial(update, k))
        return carry

    def update(k):
        a, z = k * NB, (k + 1) * NB
        w = lower[...]
        inverse[a:z, :] = w
        triangle_ref[a:z, a:z] = upper[...]
        if k:
            triangle_ref[a:z, 0:a] = jnp.zeros((NB, a), jnp.float32)
        if k + 1 < blocks:
            triangle_ref[a:z, z:p] = dot(w, gram[a:z, z:p])
        projected_ref[a:z, :] = dot(w, cross[a:z, :])
        for i in range(k + 1, blocks):
            lo, hi = i * NB, (i + 1) * NB
            left = triangle_ref[a:z, lo:hi]
            gram[lo:hi, lo:p] -= dot_t(left, triangle_ref[a:z, lo:p])
            cross[lo:hi, :] -= dot_t(left, projected_ref[a:z, :])

    lax.fori_loop(0, blocks, step, 0)
    for k in reversed(range(blocks)):
        a, z = k * NB, (k + 1) * NB
        rhs = projected_ref[a:z, :]
        if k + 1 < blocks:
            rhs = rhs - dot(triangle_ref[a:z, z:p], solved[z:p, :])
        solved[a:z, :] = dot_t(inverse[a:z, :], rhs)
    remainder_ref[...] = trailing_ref[...] - dot(panel_ref[...], solved[...])


def solve(panel_group, gram_sum, cross_sum, trailing):
    p = gram_sum.shape[0]
    n = cross_sum.shape[1]
    f32 = jnp.float32
    vmem = pl.BlockSpec(memory_space=pltpu.VMEM)
    return pl.pallas_call(
        solve_kernel,
        out_shape=(
            jax.ShapeDtypeStruct((p, p), f32),
            jax.ShapeDtypeStruct((p, n), f32),
            jax.ShapeDtypeStruct(trailing.shape, f32),
        ),
        in_specs=[vmem] * 4,
        out_specs=(vmem,) * 3,
        scratch_shapes=[
            pltpu.VMEM((p, p), f32),
            pltpu.VMEM((p, n), f32),
            pltpu.VMEM((p, NB), f32),
            pltpu.VMEM((p, n), f32),
            pltpu.VMEM((NB, NB), f32),
            pltpu.VMEM((NB, NB), f32),
            pltpu.VMEM((NB, NB), f32),
        ],
        name="factor_project",
    )(panel_group, gram_sum, cross_sum, trailing)


def on_device(panel_block, trailing):
    panel_group = lax.all_gather(panel_block, "dev", axis=0, tiled=True)
    gram_part = jnp.dot(panel_group.T, panel_group, precision=HIGHEST)
    cross_part = jnp.dot(panel_group.T, trailing, precision=HIGHEST)
    gram_sum, cross_sum = lax.psum((gram_part, cross_part), ("half", "grp"))
    return solve(panel_group, gram_sum, cross_sum, trailing)


def solution(mesh):
    placed = (P(("half", "grp", "dev"), None), P(("half", "grp"), "dev"))
    return jax.shard_map(
        on_device,
        mesh=mesh,
        in_specs=placed,
        out_specs=(P(), P(None, "dev"), P(("half", "grp"), "dev")),
        check_vma=False,
    )
```

```python
import functools

import jax
import jax.numpy as jnp
from jax import lax
from jax.experimental import pallas as pl
from jax.experimental.pallas import tpu as pltpu
from jax.sharding import PartitionSpec as P

HIGHEST = lax.Precision.HIGHEST
NB = 128
SUB = 8


def dot(a, b):
    return jnp.dot(a, b, precision=HIGHEST, preferred_element_type=jnp.float32)


def dot_t(a, b):
    return lax.dot_general(
        a, b, (((0,), (0,)), ((), ())), precision=HIGHEST,
        preferred_element_type=jnp.float32,
    )


def factor_block(block, upper_ref, inverse_ref, row0, col0):
    tile = (SUB, NB)
    lane = lax.broadcasted_iota(jnp.int32, tile, 1)
    zero = jnp.zeros(tile, jnp.float32)
    groups = len(block)
    block = list(block)
    for b in range(groups):
        c0 = SUB * b
        own = block[b]
        marks = [lane == c0 + t for t in range(SUB)]
        inside = (lane >= c0) & (lane < c0 + SUB)
        after = lane >= c0 + SUB
        rows = [jnp.broadcast_to(own[s:s + 1, :], tile) for s in range(SUB)]
        d = {}
        for s in range(SUB):
            for t in range(s, SUB):
                d[s, t] = jnp.broadcast_to(rows[s][:, c0 + t:c0 + t + 1], tile)
        columns = [
            [jnp.broadcast_to(block[g][:, c0 + t:c0 + t + 1], tile) for t in range(SUB)]
            for g in range(b + 1, groups)
        ]
        v = []
        for s in range(SUB):
            unit = jnp.where(marks[s], 1.0, 0.0)
            v.append(jnp.where(inside, unit, rows[s]))
        for j in range(SUB):
            rs = lax.rsqrt(d[j, j])
            u = {k: d[j, k] * rs for k in range(j, SUB)}
            vs = v[j] * rs
            up = jnp.where(after, vs, zero)
            for k in range(j, SUB):
                up = jnp.where(marks[k], u[k], up)
            low = jnp.where(after, zero, vs)
            upper_ref[row0 + c0 + j:row0 + c0 + j + 1, col0:col0 + NB] = up[0:1, :]
            inverse_ref[row0 + c0 + j:row0 + c0 + j + 1, :] = low[0:1, :]
            for i in range(SUB):
                if i == j:
                    continue
                e = u[i] if i > j else d[i, j] * rs
                v[i] = v[i] - e * vs
                for k in range(max(j + 1, i), SUB):
                    d[i, k] = d[i, k] - e * u[k]
            v[j] = vs * rs
            for k in range(j + 1, SUB):
                d[j, k] = u[k] * rs
        for g in range(b + 1, groups):
            terms = [columns[g - b - 1][t] * v[t] for t in range(SUB)]
            while len(terms) > 1:
                terms = [terms[i] + terms[i + 1] for i in range(0, len(terms), 2)]
            block[g] = jnp.where(inside, zero, block[g]) - terms[0]


def solve_kernel(panel_ref, packed_ref, trailing_ref, triangle_ref, projected_ref,
                 remainder_ref, gram, cross, inverse, solved, corner, upper, lower):
    p = panel_ref.shape[1]
    blocks = p // NB
    for (i, j), at in packing(p, trailing_ref.shape[1]).items():
        part = packed_ref[at:at + NB, :]
        if j < blocks:
            gram[i * NB:(i + 1) * NB, j * NB:(j + 1) * NB] = part
        else:
            cross[i * NB:(i + 1) * NB, (j - blocks) * NB:(j - blocks + 1) * NB] = part
    def step(index, carry):
        start = pl.multiple_of(index * NB, NB)
        corner[...] = gram[pl.ds(start, NB), pl.ds(start, NB)]
        rows = [corner[SUB * g:SUB * (g + 1), :] for g in range(NB // SUB)]
        factor_block(rows, upper, lower, 0, 0)
        for k in range(blocks):
            pl.when(index == k)(functools.partial(update, k))
        return carry

    def update(k):
        a, z = k * NB, (k + 1) * NB
        w = lower[...]
        inverse[a:z, :] = w
        triangle_ref[a:z, a:z] = upper[...]
        if k:
            triangle_ref[a:z, 0:a] = jnp.zeros((NB, a), jnp.float32)
        if k + 1 < blocks:
            triangle_ref[a:z, z:p] = dot(w, gram[a:z, z:p])
        projected_ref[a:z, :] = dot(w, cross[a:z, :])
        for i in range(k + 1, blocks):
            lo, hi = i * NB, (i + 1) * NB
            left = triangle_ref[a:z, lo:hi]
            gram[lo:hi, lo:p] -= dot_t(left, triangle_ref[a:z, lo:p])
            cross[lo:hi, :] -= dot_t(left, projected_ref[a:z, :])

    lax.fori_loop(0, blocks, step, 0)
    for k in reversed(range(blocks)):
        a, z = k * NB, (k + 1) * NB
        rhs = projected_ref[a:z, :]
        if k + 1 < blocks:
            rhs = rhs - dot(triangle_ref[a:z, z:p], solved[z:p, :])
        solved[a:z, :] = dot_t(inverse[a:z, :], rhs)
    remainder_ref[...] = trailing_ref[...] - dot(panel_ref[...], solved[...])


def solve(panel_group, packed, trailing):
    p = panel_group.shape[1]
    n = trailing.shape[1]
    f32 = jnp.float32
    vmem = pl.BlockSpec(memory_space=pltpu.VMEM)
    return pl.pallas_call(
        solve_kernel,
        out_shape=(
            jax.ShapeDtypeStruct((p, p), f32),
            jax.ShapeDtypeStruct((p, n), f32),
            jax.ShapeDtypeStruct(trailing.shape, f32),
        ),
        in_specs=[vmem] * 3,
        out_specs=(vmem,) * 3,
        scratch_shapes=[
            pltpu.VMEM((p, p), f32),
            pltpu.VMEM((p, n), f32),
            pltpu.VMEM((p, NB), f32),
            pltpu.VMEM((p, n), f32),
            pltpu.VMEM((NB, NB), f32),
            pltpu.VMEM((NB, NB), f32),
            pltpu.VMEM((NB, NB), f32),
        ],
        name="factor_project",
    )(panel_group, packed, trailing)


def packing(p, n):
    blocks = p // NB
    where = {}
    for i in range(blocks):
        for j in range(i, blocks):
            where[i, j] = len(where) * NB
    for i in range(blocks):
        for j in range(n // NB):
            where[i, blocks + j] = len(where) * NB
    return where


def gather_kernel(halves, groups, devs, panel_ref, trailing_ref, group_ref, packed_ref, panel,
                  total, inbox, a_send, a_recv, b_send, b_recv, r_send, r_recv):
    mesh_ids = pl.DeviceIdType.MESH
    mine = lax.axis_index("dev")
    rank = lax.axis_index("half") * groups + lax.axis_index("grp")
    pairs = devs // 2
    pair, parity = mine // 2, mine % 2
    levels = (halves * groups).bit_length() - 1
    rows, p = panel_ref.shape
    n = trailing_ref.shape[1]
    blocks = p // NB

    def slot(dev):
        return pl.ds(pl.multiple_of(dev * rows, rows), rows)

    def same(step):
        return ((pair + step) % pairs) * 2 + parity

    def at_rank(level):
        bit = 1 << level
        other = rank + bit * (1 - 2 * ((rank // bit) % 2))
        return {"half": other // groups, "grp": other % groups}

    beside = pair * 2 + 1 - parity
    peers = [{"dev": same(step)} for step in range(1, pairs)] + [{"dev": beside}]
    peers += [at_rank(level) for level in range(levels)]
    barrier = pltpu.get_barrier_semaphore()
    for peer in peers:
        pl.semaphore_signal(barrier, inc=1, device_id=peer, device_id_type=mesh_ids)
    pl.semaphore_wait(barrier, len(peers))

    first = [
        pltpu.make_async_remote_copy(
            src_ref=panel_ref, dst_ref=panel.at[slot(mine)], send_sem=a_send.at[step],
            recv_sem=a_recv.at[step], device_id={"dev": same(step)}, device_id_type=mesh_ids)
        for step in range(1, pairs)
    ]
    onward = []
    for step in range(pairs):
        owner = same(pairs - step)
        onward.append(pltpu.make_async_remote_copy(
            src_ref=panel.at[slot(owner)] if step else panel_ref,
            dst_ref=panel.at[slot(owner)], send_sem=b_send.at[step],
            recv_sem=b_recv.at[step], device_id={"dev": beside}, device_id_type=mesh_ids))
    for copy in first:
        copy.start()
    onward[0].start()
    panel[slot(mine), :] = panel_ref[...]
    for step in range(1, pairs):
        first[step - 1].wait_recv()
        onward[step].start()
    for copy in onward:
        copy.wait_recv()

    where = packing(p, n)
    for i in range(blocks):
        left = panel[:, i * NB:(i + 1) * NB]
        strip = dot_t(left, panel[:, i * NB:p])
        for j in range(i, blocks):
            at = where[i, j]
            total[at:at + NB, :] = strip[:, (j - i) * NB:(j - i + 1) * NB]
    crossed = dot_t(panel[...], trailing_ref[...])
    for i in range(blocks):
        for j in range(n // NB):
            at = where[i, blocks + j]
            total[at:at + NB, :] = crossed[i * NB:(i + 1) * NB, j * NB:(j + 1) * NB]

    half = total.shape[0] // 2
    low = (rank % 2) * half
    keep = pl.ds(pl.multiple_of(low, 8), half)
    give = pl.ds(pl.multiple_of(half - low, 8), half)
    for level in range(levels):
        copy = pltpu.make_async_remote_copy(
            src_ref=total.at[keep if level else give], dst_ref=inbox.at[level],
            send_sem=r_send.at[level], recv_sem=r_recv.at[level],
            device_id=at_rank(level), device_id_type=mesh_ids)
        copy.start()
        if level == 0:
            group_ref[...] = panel[...]
        copy.wait()
        total[keep, :] += inbox[level]
    back = pltpu.make_async_remote_copy(
        src_ref=total.at[keep], dst_ref=inbox.at[levels],
        send_sem=r_send.at[levels], recv_sem=r_recv.at[levels],
        device_id=at_rank(0), device_id_type=mesh_ids)
    back.start()
    packed_ref[keep, :] = total[keep, :]
    for copy in first + onward:
        copy.wait_send()
    back.wait()
    packed_ref[give, :] = inbox[levels]


def gather_reduce(mesh, panel_block, trailing):
    halves, groups, devs = (mesh.shape[name] for name in ("half", "grp", "dev"))
    rows, p = panel_block.shape
    n = trailing.shape[1]
    f32 = jnp.float32
    size = len(packing(p, n)) * NB
    levels = (halves * groups).bit_length() - 1
    vmem = pl.BlockSpec(memory_space=pltpu.VMEM)
    dma = pltpu.SemaphoreType.DMA
    return pl.pallas_call(
        functools.partial(gather_kernel, halves, groups, devs),
        out_shape=(
            jax.ShapeDtypeStruct((rows * devs, p), f32),
            jax.ShapeDtypeStruct((size, NB), f32),
        ),
        in_specs=[vmem] * 2,
        out_specs=(vmem,) * 2,
        scratch_shapes=[
            pltpu.VMEM((rows * devs, p), f32),
            pltpu.VMEM((size, NB), f32),
            pltpu.VMEM((levels + 1, size // 2, NB), f32),
            dma((devs // 2,)), dma((devs // 2,)), dma((devs // 2,)), dma((devs // 2,)),
            dma((levels + 1,)), dma((levels + 1,)),
        ],
        compiler_params=pltpu.CompilerParams(collective_id=0, has_side_effects=True),
        name="gather_reduce",
    )(panel_block, trailing)


def on_device(mesh, panel_block, trailing):
    panel_group, packed = gather_reduce(mesh, panel_block, trailing)
    return solve(panel_group, packed, trailing)


def solution(mesh):
    placed = (P(("half", "grp", "dev"), None), P(("half", "grp"), "dev"))
    return jax.shard_map(
        functools.partial(on_device, mesh),
        mesh=mesh,
        in_specs=placed,
        out_specs=(P(), P(None, "dev"), P(("half", "grp"), "dev")),
        check_vma=False,
    )
```
